32 devices in a mesh: blk: 2 (over y), visit: 4 (over z), patch: 2 (over x), row: 2 (over core).
Axes of the slice: x: 2, y: 2, z: 4, core: 2. Of those that a mesh axis runs over, the one named last changes fastest.
Arguments:
- exposures: bfloat16 [8, 4, 256, 4096], P(('blk', 'visit'), 'patch', 'row'), parts along dimension 0, may hold values from -6 to 6
- kernel_choice: int32 [8, 4], P(('blk', 'visit'), 'patch'), parts along dimension 0, may hold values from 0 to 15
- kernel_coeffs: float32 [9, 16], replicated, may hold values from -2 to 2
- row_taps: bfloat16 [9, 21], replicated, may hold values from -1.25 to 1.25
- column_taps: bfloat16 [9, 21], replicated, may hold values from -1.25 to 1.25
- visit_weight: bfloat16 [8, 4], P('blk'), parts along dimension 0, may hold values from 0.29882812 to 3
- footprints: int32 [3, 8, 2, 32], P(None, 'blk', 'patch'), parts along dimension 1, may hold values from -1 to 3967, as said below
- star_coeffs: float32 [4, 32, 2048], P(('blk', 'patch'), None, ('visit', 'row')), parts along dimension 0, may hold values from -180 to 180
Outputs:
- coadd: float32 [4, 8, 256, 128], P(('blk', 'patch'), 'visit', 'row'), parts along dimension 0
- psf_factor: float32 [4, 32, 32], P(('blk', 'patch')), parts along dimension 0
- whitened: float32 [4, 32, 2048], P(('blk', 'patch'), None, ('visit', 'row')), parts along dimension 0
The draws below stay inside these ranges and needn't reach their ends.
There are 2 independent parts, one for each index of `blk`. The reference program is written for one: setup_inputs(seed, part) draws one part's arguments, and reference() takes and returns one part's arrays. A program takes and returns all parts, laid end to end along the dimension named above; an argument that names none is the same for every part. Nothing has to cross between parts.
Inputs may be any that keep to these rules, and one draw needn't show every extreme that they name: `footprints`: for source visit index s, patch p and entry q: field 0 is the source block k of visit s + k // 2 and CCD p * 2 + k % 2, or -1 for an empty entry; field 1 is the column offset, at most 3967; field 2 the tile slot, 0 to 1. Entry q goes to the owner with visit index q // 8, so at most 8 entries pass from one source to one owner, and in every patch one owner receives 8 live entries from every source. Every tile slot of every owner receives at least one live entry. Empty entries hold 0 in fields 1 and 2.
All inputs are finite; a program needn't handle non-finite values.
Results may differ from the reference program's by a relative error of at most 0.007.
Values may be sent and summed in bfloat16 or wider, within the bound.
A program may use at most 192 MiB of HBM per device.

```python
import math
from functools import partial
import jax
import jax.numpy as jnp
from jax import lax

TAPS = 21
NBASIS = 9
NCOEF = 16
NCOMP = 32
V_DEV = 1
C_DEV = 2
CW = 4096
TW = 128
CAP = 8
TILES_DEV = 2
HALF = 10
SOURCES = 4
PATCHES = 2
VISITS = 4
CCDS = 4
CROWS = 256
SLABS = 2
SLOTS = 32
TILES = 8
STARS = 2048


def draw_footprints(key, part):
    subkeys = jax.random.split(key, 5)
    full_shape = (SOURCES, PATCHES, SLOTS)
    busiest = jax.random.randint(subkeys[0], (1, PATCHES, 1), 0, SOURCES)
    source = jnp.arange(SOURCES, dtype=jnp.int32)[:, None, None]
    target = (jnp.arange(SLOTS, dtype=jnp.int32) // CAP)[None, None, :]
    lane_index = (jnp.arange(SLOTS, dtype=jnp.int32) % CAP)[None, None, :]
    covering = jnp.broadcast_to(source == (target + 1) % SOURCES, full_shape)
    chosen = jax.random.randint(subkeys[1], full_shape, 0, 3) == 0
    hole = (source == busiest) & (target == (busiest + 2) % SOURCES) & (lane_index == CAP - 1)
    live_mask = ((target == busiest) | covering | chosen) & jnp.logical_not(hole)
    corner = (source == 0) & (target == busiest) & (lane_index == 0)
    slab_ids = jnp.where(corner, SLABS - 1, jax.random.randint(subkeys[2], full_shape, 0, SLABS))
    offsets = jnp.where(corner, CW - TW - 1, jax.random.randint(subkeys[3], full_shape, 0, CW - TW))
    slot_ids = jnp.where(covering, jnp.broadcast_to(lane_index % TILES_DEV, full_shape), jax.random.randint(subkeys[4], full_shape, 0, TILES_DEV))
    slab_ids = jnp.where(live_mask, slab_ids, -1)
    offsets = jnp.where(live_mask, offsets, 0)
    slot_ids = jnp.where(live_mask, slot_ids, 0)
    return jnp.stack([slab_ids, offsets, slot_ids]).astype(jnp.int32)


def draw_star_coeffs(key, part):
    subkeys = jax.random.split(key, 3)
    position = jnp.arange(STARS, dtype=jnp.float32) / STARS
    row_scale = jnp.exp(jnp.log(10.0) * jax.random.uniform(subkeys[1], (PATCHES, 1, STARS))) * jnp.power(3.0, position)
    column_scale = jnp.exp(jnp.log(10.0) * jax.random.uniform(subkeys[2], (PATCHES, NCOMP, 1)))
    entries = jnp.clip(jax.random.normal(subkeys[0], (PATCHES, NCOMP, STARS)), -6.0, 6.0)
    return (0.1 * entries * row_scale * column_scale).astype(jnp.float32)


def touch_ends(values, rng, smallest, largest):
    longest = values.shape.index(max(values.shape))
    spots = []
    for shift in (0, 1):
        where = [jax.random.randint(jax.random.fold_in(rng, axis), (), 0, length) for axis, length in enumerate(values.shape)]
        where[longest] = (where[longest] + shift) % values.shape[longest]
        spots.append(tuple(where))
    return values.at[spots[0]].set(smallest).at[spots[1]].set(largest)


def block_scale(stream_key, shape, pieces, least, high):
    loudness = 1.0
    for dim, blocks in pieces:
        steps = jax.random.uniform(jax.random.fold_in(jax.random.fold_in(stream_key, 6), dim), (blocks,), jnp.float32, least / len(pieces), high / len(pieces))
        loudness = loudness * jnp.repeat(jnp.exp(steps), shape[dim] // blocks).reshape((-1,) + (1,) * (len(shape) - 1 - dim))
    return loudness


def noise(stream_key, shape, scale, most, cuts=(), held_as=jnp.bfloat16):
    array = scale * jax.random.normal(stream_key, shape, jnp.float32)
    if cuts:
        array = array * block_scale(stream_key, shape, cuts, -0.22, 0.18)
    return jnp.clip(array, -most, most).astype(held_as)


def setup_inputs(seed: int = 0, part: int = 0) -> dict:
    key_of = jax.random.split(jax.random.key(seed), 9)
    own_keys = jax.random.split(jax.random.fold_in(key_of[8], part), 9)
    return {
        "exposures": noise(own_keys[0], (VISITS, CCDS, CROWS, CW), 1.0, 6.0, ((0, 4), (1, 2), (2, 2))),
        "kernel_choice": touch_ends(jax.random.randint(own_keys[1], (VISITS, CCDS), 0, NCOEF), jax.random.fold_in(own_keys[1], 1), 0, NCOEF - 1).astype(jnp.int32),
        "kernel_coeffs": noise(key_of[2], (NBASIS, NCOEF), NBASIS ** -0.5, 2.0, (), jnp.float32),
        "row_taps": noise(key_of[3], (NBASIS, TAPS), TAPS ** -0.5, 1.25),
        "column_taps": noise(key_of[4], (NBASIS, TAPS), TAPS ** -0.5, 1.25),
        "visit_weight": jnp.clip(jnp.exp(jax.random.uniform(own_keys[5], (VISITS, CCDS), jnp.float32, math.log(0.29882812), math.log(3.0))), 0.29882812, 3.0).astype(jnp.bfloat16),
        "footprints": draw_footprints(jax.random.fold_in(jax.random.fold_in(key_of[8], part), 71), part),
        "star_coeffs": draw_star_coeffs(jax.random.fold_in(jax.random.fold_in(key_of[8], part), 71), part),
    }


HIGHEST = lax.Precision.HIGHEST
BILINEAR = (0.28125, 0.46875, 0.09375, 0.15625)

def match_image(operands, column_taps):
    image, mixing = operands
    padded = jnp.pad(image.astype(jnp.float32), ((0, 0), (HALF, HALF)))
    shifted = jnp.stack([padded[:, offset:offset + CW] for offset in range(TAPS)])
    filtered = jnp.einsum('bt,trc->brc', column_taps.astype(jnp.float32), shifted, precision=HIGHEST).astype(jnp.bfloat16)
    padded_rows = jnp.pad(filtered.astype(jnp.float32), ((0, 0), (HALF, HALF), (0, 0)))
    stacked = jnp.stack([padded_rows[:, offset:offset + CROWS, :] for offset in range(TAPS)], axis=1)
    summed = jnp.einsum('bt,btrc->rc', mixing.astype(jnp.float32), stacked, precision=HIGHEST)
    return summed.astype(jnp.bfloat16)

def reference(exposures, kernel_choice, kernel_coeffs, row_taps, column_taps, visit_weight, footprints, star_coeffs):
    gram = jnp.einsum('pks,pls->pkl', star_coeffs, star_coeffs, precision=HIGHEST)
    psf_factor = jnp.linalg.cholesky(gram) / math.sqrt(STARS)
    whitened = lax.linalg.triangular_solve(psf_factor, star_coeffs, left_side=True, lower=True)
    factor_diag = jnp.diagonal(psf_factor, axis1=1, axis2=2)[:, :NBASIS]
    basis_scale = factor_diag / jnp.sqrt(lax.optimization_barrier(jnp.mean(factor_diag * factor_diag, axis=1, keepdims=True)))
    ccd_scale = jnp.repeat(basis_scale, C_DEV, axis=0)
    coefficient = jnp.transpose(kernel_coeffs)[kernel_choice] * ccd_scale[None]
    mixing = (coefficient[..., None] * row_taps.astype(jnp.float32)).astype(jnp.bfloat16)
    images = exposures.reshape(VISITS * CCDS, CROWS, CW)
    mixes = mixing.reshape(VISITS * CCDS, NBASIS, TAPS)
    matched = lax.map(partial(match_image, column_taps=column_taps), (images, mixes))
    matched = jnp.pad(matched.reshape(VISITS, CCDS, CROWS, CW), ((0, 0), (0, 0), (0, 1), (0, 0)))
    patch_ids = jnp.arange(PATCHES, dtype=jnp.int32)[:, None]
    tile_ids = jnp.arange(TILES, dtype=jnp.int32)
    target_base = jnp.arange(SLOTS, dtype=jnp.int32) // CAP * TILES_DEV

    def cut_window(visit_id, ccd_id, offset):
        return lax.dynamic_slice(matched, (visit_id, ccd_id, jnp.int32(0), offset), (1, 1, CROWS + 1, TW + 1))[0, 0]

    def add_source(carry, source):
        numerator, totals = carry
        fields = lax.dynamic_index_in_dim(footprints, source, axis=1, keepdims=False)
        slab_ids = fields[0]
        safe_ids = jnp.maximum(slab_ids, 0)
        visit_ids = (source * V_DEV + safe_ids // C_DEV).astype(jnp.int32)
        ccd_ids = (patch_ids * C_DEV + safe_ids % C_DEV).astype(jnp.int32)
        windows = jax.vmap(jax.vmap(cut_window))(visit_ids, ccd_ids, fields[1].astype(jnp.int32)).astype(jnp.float32)
        warped = (BILINEAR[0] * windows[:, :, :-1, :-1] + BILINEAR[1] * windows[:, :, :-1, 1:] + BILINEAR[2] * windows[:, :, 1:, :-1] + BILINEAR[3] * windows[:, :, 1:, 1:]).astype(jnp.bfloat16)
        weights = jnp.where(slab_ids >= 0, visit_weight[visit_ids, ccd_ids].astype(jnp.float32), 0.0)
        targets = target_base[None, :] + fields[2]
        spread = jnp.where(targets[:, :, None] == tile_ids, weights[:, :, None], 0.0)
        contribution = jnp.einsum('pqg,pqrc->pgrc', spread, warped.astype(jnp.float32), precision=HIGHEST)
        contribution = lax.optimization_barrier(contribution.astype(jnp.bfloat16)).astype(jnp.float32)
        numerator = numerator + contribution
        totals = totals + lax.optimization_barrier(jnp.sum(spread, axis=1))
        return ((numerator, totals), None)
    start = (jnp.zeros((PATCHES, TILES, CROWS, TW), jnp.float32), jnp.zeros((PATCHES, TILES), jnp.float32))
    (numerator, totals), unused = lax.scan(add_source, start, jnp.arange(SOURCES, dtype=jnp.int32))
    coadd = numerator / totals[:, :, None, None]
    return (coadd, psf_factor, whitened)
```

```python
import functools
import math

import jax
import jax.numpy as jnp
from jax import lax
from jax.experimental import pallas as pl
from jax.experimental.pallas import tpu as pltpu
from jax.sharding import PartitionSpec as P

NBASIS = 9
NTAPS = 21
C_DEV = 2
R_DEV = 128
CW = 4096
TW = 128
CAP = 8
TILES_DEV = 2
HALF = 10
SLABS = 2
HALO = 16
EXT = R_DEV + HALO
NCOMP = 32
BK = NBASIS * EXT
PAD = 128
HIGHEST = lax.Precision.HIGHEST
VMEM_LIMIT = 60 * 1024 * 1024


def blended(taps, near, far):
    zero = jnp.zeros((taps.shape[0], 1), jnp.float32)
    taps = taps.astype(jnp.float32)
    return near * jnp.concatenate([taps, zero], 1) + far * jnp.concatenate([zero, taps], 1)


def column_band(taps):
    both = blended(taps, 0.375, 0.625)
    diff = jnp.arange(2 * TW)[:, None] - jnp.arange(TW)[None, :]
    picks = (diff[None] == jnp.arange(NTAPS + 1)[:, None, None]).astype(jnp.float32)
    out = jnp.einsum("bt,tuw->ubw", both, picks, precision=HIGHEST)
    return out.reshape(2 * TW, NBASIS * TW).astype(jnp.bfloat16)


def row_band(taps, row_index):
    e = jnp.arange(EXT)
    position = jnp.where(e < R_DEV, e, jnp.where(row_index == 0, e, e - EXT))
    diff = position[None, :] - jnp.arange(R_DEV)[:, None] + HALF
    steps = jnp.arange(NTAPS)[:, None, None]
    last = (jnp.arange(R_DEV)[:, None] == R_DEV - 1) & (row_index == 1)
    picks = 0.75 * (diff[None] == steps) + jnp.where(last[None], 0.0, 0.25) * (diff[None] - 1 == steps)
    out = jnp.einsum("bt,tie->ibe", taps.astype(jnp.float32), picks, precision=HIGHEST)
    return out.reshape(R_DEV, BK)


def window_kernel(entry_ref, image_ref, halo_ref, band_ref, z_ref, padded, sums):
    slots = entry_ref.shape[1]
    groups = slots // CAP * TILES_DEV
    for k in range(SLABS):
        padded[k, :, 0:PAD] = jnp.zeros((EXT, PAD), jnp.bfloat16)
        padded[k, :, PAD + CW :] = jnp.zeros((EXT, PAD), jnp.bfloat16)
        padded[k, 0:R_DEV, PAD : PAD + CW] = image_ref[k]
        padded[k, R_DEV:EXT, PAD : PAD + CW] = halo_ref[k]
    sums[...] = jnp.zeros_like(sums)
    lane = lax.broadcasted_iota(jnp.int32, (EXT, TW), 1)

    @pl.loop(0, slots)
    def _(q):
        k = entry_ref[0, q]

        @pl.when(k >= 0)
        def _():
            start = entry_ref[1, q] + (PAD - HALF)
            tile = lax.shift_right_logical(start, 7)
            shift = start - tile * TW
            back = jnp.where(shift == 0, 0, TW - shift)
            group = (q // CAP) * TILES_DEV + entry_ref[2, q]
            parts = []
            for t in range(3):
                at = pl.multiple_of((tile + t) * TW, TW)
                part = padded[k, :, pl.ds(at, TW)].astype(jnp.float32)
                parts.append(pltpu.roll(part, back, 1))
            keep = lane < TW - shift
            slot = group * SLABS + k
            sums[slot, :, 0:TW] += jnp.where(keep, parts[0], parts[1])
            sums[slot, :, TW : 2 * TW] += jnp.where(keep, parts[1], parts[2])

    @pl.loop(0, groups)
    def _(g):
        for k in range(SLABS):
            window = sums[g * SLABS + k].astype(jnp.bfloat16)
            out = jnp.dot(window, band_ref[...], preferred_element_type=jnp.float32)
            out = out.astype(jnp.bfloat16)
            for b in range(NBASIS):
                row = (k * NBASIS + b) * EXT
                z_ref[row : row + EXT, pl.ds(pl.multiple_of(g * TW, TW), TW)] = out[
                    :, b * TW : (b + 1) * TW
                ]


def factor_steps(gram, stars):
    sub = lax.broadcasted_iota(jnp.int32, (NCOMP, 1), 0)
    lane = lax.broadcasted_iota(jnp.int32, (NCOMP, NCOMP), 1)
    lower = jnp.zeros((NCOMP, NCOMP), jnp.float32)
    for j in range(NCOMP):
        inv = 1.0 / jnp.sqrt(gram[j : j + 1, j : j + 1])
        column = gram[:, j : j + 1] * inv
        lower = jnp.where((lane == j) & (sub >= j), column, lower)
        below = jnp.where(sub > j, column, 0.0)
        solved = stars[j : j + 1, :] * inv
        gram = gram - below * (gram[j : j + 1, :] * inv)
        stars = jnp.where(sub == j, solved, stars - below * solved)
    return lower, stars


def mix_kernel(
    star_total,
    choice_ref,
    weight_ref,
    gram_ref,
    star_ref,
    coeff_ref,
    rows_ref,
    z_ref,
    partial_ref,
    factor_ref,
    white_ref,
):
    gram = gram_ref[0]
    for s in range(1, gram_ref.shape[0]):
        gram = gram + gram_ref[s]
    lower, solved = factor_steps(gram, star_ref[...])
    root = math.sqrt(star_total)
    factor = lower / root
    factor_ref[...] = factor
    white_ref[...] = solved * root
    eye = lax.broadcasted_iota(jnp.int32, (NCOMP, NCOMP), 0) == lax.broadcasted_iota(
        jnp.int32, (NCOMP, NCOMP), 1
    )
    diag = jnp.sum(jnp.where(eye, factor, 0.0), axis=1, keepdims=True)[:NBASIS]
    scale = diag / jnp.sqrt(jnp.sum(diag * diag, axis=0, keepdims=True) / NBASIS)
    column = lax.broadcasted_iota(jnp.int32, (NBASIS, BK), 1)
    first = lax.broadcasted_iota(jnp.int32, (NBASIS, BK), 0) * EXT
    spread = (column >= first) & (column < first + EXT)
    sets = lax.broadcasted_iota(jnp.int32, coeff_ref.shape, 1)
    total = None
    for k in range(SLABS):
        picked = jnp.sum(
            jnp.where(sets == choice_ref[k], coeff_ref[...], 0.0), axis=1, keepdims=True
        )
        by_row = picked * scale * weight_ref[k]
        vector = jnp.sum(jnp.where(spread, by_row, 0.0), axis=0, keepdims=True)
        mixed = (rows_ref[...] * vector).astype(jnp.bfloat16)
        term = jnp.dot(
            mixed, z_ref[k * BK : (k + 1) * BK, :], preferred_element_type=jnp.float32
        )
        total = term if total is None else total + term
    for g in range(partial_ref.shape[0]):
        partial_ref[g] = total[:, g * TW : (g + 1) * TW].astype(jnp.bfloat16)


def on_device(
    exposures,
    kernel_choice,
    kernel_coeffs,
    row_taps,
    column_taps,
    visit_weight,
    footprints,
    star_coeffs,
):
    stars = star_coeffs[0]
    row_index = lax.axis_index("row")
    source_index = lax.axis_index("visit")
    patch_index = lax.axis_index("patch")
    sources = footprints.shape[1]
    groups = sources * TILES_DEV
    star_total = stars.shape[1] * lax.axis_size("visit") * lax.axis_size("row")
    gram = jnp.dot(stars, stars.T, precision=HIGHEST, preferred_element_type=jnp.float32)
    grams = lax.all_gather(gram, ("visit", "row"))
    images = exposures.reshape(SLABS, R_DEV, CW)
    edge = jnp.where(row_index == 0, images[:, R_DEV - HALO :], images[:, :HALO])
    halo = lax.ppermute(edge, "row", [(0, 1), (1, 0)])
    own_list = footprints[:, :, 0, :]
    entries = lax.dynamic_index_in_dim(own_list, source_index, axis=1, keepdims=False)
    vmem = pl.BlockSpec(memory_space=pltpu.VMEM)
    smem = pl.BlockSpec(memory_space=pltpu.SMEM)
    z = pl.pallas_call(
        window_kernel,
        out_shape=jax.ShapeDtypeStruct((SLABS * BK, groups * TW), jnp.bfloat16),
        in_specs=[smem, vmem, vmem, vmem],
        out_specs=vmem,
        scratch_shapes=[
            pltpu.VMEM((SLABS, EXT, CW + 2 * PAD), jnp.bfloat16),
            pltpu.VMEM((groups * SLABS, EXT, 2 * TW), jnp.float32),
        ],
        compiler_params=pltpu.CompilerParams(vmem_limit_bytes=VMEM_LIMIT),
        cost_estimate=pl.CostEstimate(flops=2 * 10**9, bytes_accessed=10**7, transcendentals=0),
        name="windows",
    )(entries, images, halo, column_band(column_taps))
    table = visit_weight.astype(jnp.float32)
    own_weight = lax.dynamic_slice(
        table, (source_index, patch_index * C_DEV), (1, C_DEV)
    ).reshape(C_DEV)
    partial, factor, whitened = pl.pallas_call(
        functools.partial(mix_kernel, star_total),
        out_shape=(
            jax.ShapeDtypeStruct((groups, R_DEV, TW), jnp.bfloat16),
            jax.ShapeDtypeStruct((NCOMP, NCOMP), jnp.float32),
            jax.ShapeDtypeStruct(stars.shape, jnp.float32),
        ),
        in_specs=[smem, smem, vmem, vmem, vmem, vmem, vmem],
        out_specs=(vmem, vmem, vmem),
        compiler_params=pltpu.CompilerParams(vmem_limit_bytes=VMEM_LIMIT),
        name="mix",
    )(
        kernel_choice.reshape(SLABS),
        own_weight,
        grams,
        stars,
        kernel_coeffs,
        row_band(row_taps, row_index),
        z,
    )
    incoming = lax.dynamic_slice_in_dim(own_list, source_index * CAP, CAP, axis=2)
    own_table = lax.dynamic_slice_in_dim(table, patch_index * C_DEV, C_DEV, axis=1)
    per_entry = jnp.where(
        incoming[0] < 0,
        0.0,
        jnp.where(incoming[0] == 0, own_table[:, 0:1], own_table[:, 1:2]),
    )
    tile_ids = jnp.arange(TILES_DEV, dtype=jnp.int32)[:, None, None]
    totals = jnp.sum(jnp.where(incoming[2][None] == tile_ids, per_entry[None], 0.0), axis=(1, 2))
    outgoing = partial.reshape(sources, TILES_DEV, R_DEV, TW)
    received = lax.all_to_all(outgoing, "visit", split_axis=0, concat_axis=0, tiled=True)
    numerator = jnp.sum(received.astype(jnp.float32), axis=0)
    coadd = (numerator / totals[:, None, None])[None]
    return (coadd, factor[None], whitened[None])


def solution(mesh):
    in_specs = (
        P(("blk", "visit"), "patch", "row", None),
        P(("blk", "visit"), "patch"),
        P(),
        P(),
        P(),
        P("blk", None),
        P(None, "blk", "patch", None),
        P(("blk", "patch"), None, ("visit", "row")),
    )
    out_specs = (
        P(("blk", "patch"), "visit", "row", None),
        P(("blk", "patch"), None, None),
        P(("blk", "patch"), None, ("visit", "row")),
    )
    return jax.shard_map(
        on_device, mesh=mesh, in_specs=in_specs, out_specs=out_specs, check_vma=False
    )
```

```python
import functools
import math

import jax
import jax.numpy as jnp
from jax import lax
from jax.experimental import pallas as pl
from jax.experimental.pallas import tpu as pltpu
from jax.sharding import PartitionSpec as P

NBASIS = 9
NTAPS = 21
C_DEV = 2
R_DEV = 128
CW = 4096
TW = 128
CAP = 8
TILES_DEV = 2
HALF = 10
SLABS = 2
HALO = 16
NCOMP = 32
PAD = 128
PAIRS = SLABS * NBASIS
OWN_K = PAIRS * R_DEV
HALO_TILES = 3
ALL_K = OWN_K + HALO_TILES * TW
HIGHEST = lax.Precision.HIGHEST
VMEM_LIMIT = 60 * 1024 * 1024
MESH = pl.DeviceIdType.MESH


def iota(shape, axis):
    return lax.broadcasted_iota(jnp.int32, shape, axis)


def window_kernel(list_ref, image_ref, sum_ref, padded, sums, sem):
    visit = lax.axis_index("visit")
    slots = list_ref.shape[3]
    loads = []
    for k in range(SLABS):
        copy = pltpu.make_async_copy(image_ref.at[0, k], padded.at[k, :, PAD : PAD + CW], sem.at[k])
        copy.start()
        loads.append(copy)
    for k in range(SLABS):
        padded[k, :, 0:PAD] = jnp.zeros((R_DEV, PAD), jnp.bfloat16)
        padded[k, :, PAD + CW :] = jnp.zeros((R_DEV, PAD), jnp.bfloat16)
    sums[...] = jnp.zeros_like(sums)
    lane = iota((R_DEV, TW), 1)
    for copy in loads:
        copy.wait()

    @pl.loop(0, slots)
    def _(q):
        k = list_ref[0, visit, 0, q]

        @pl.when(k >= 0)
        def _():
            start = list_ref[1, visit, 0, q] + (PAD - HALF)
            tile = lax.shift_right_logical(start, 7)
            shift = start - tile * TW
            back = jnp.bitwise_and(TW - shift, TW - 1)
            place = (lax.div(q, CAP) * TILES_DEV + list_ref[2, visit, 0, q]) * SLABS + k
            parts = []
            for t in range(3):
                at = pl.multiple_of((tile + t) * TW, TW)
                parts.append(pltpu.roll(padded[k, :, pl.ds(at, TW)].astype(jnp.float32), back, 1))
            keep = lane < TW - shift
            sums[place, :, 0:TW] += jnp.where(keep, parts[0], parts[1])
            sums[place, :, TW : 2 * TW] += jnp.where(keep, parts[1], parts[2])

    @pl.loop(0, sums.shape[0])
    def _(place):
        sum_ref[place] = sums[place].astype(jnp.bfloat16)


def factor_steps(gram, stars):
    sub = lax.broadcasted_iota(jnp.int32, (NCOMP, 1), 0)
    lane = lax.broadcasted_iota(jnp.int32, (NCOMP, NCOMP), 1)
    lower = jnp.zeros((NCOMP, NCOMP), jnp.float32)
    for j in range(NCOMP):
        inv = 1.0 / jnp.sqrt(gram[j : j + 1, j : j + 1])
        column = gram[:, j : j + 1] * inv
        lower = jnp.where((lane == j) & (sub >= j), column, lower)
        below = jnp.where(sub > j, column, 0.0)
        solved = stars[j : j + 1, :] * inv
        gram = gram - below * (gram[j : j + 1, :] * inv)
        stars = jnp.where(sub == j, solved, stars - below * solved)
    return lower, stars


def fused_kernel(
    visits,
    rows_count,
    star_total,
    choice_ref,
    list_vec,
    weight_ref,
    coeff_ref,
    row_tap_ref,
    column_tap_ref,
    star_ref,
    sum_ref,
    coadd_ref,
    factor_ref,
    white_ref,
    halo,
    band,
    z,
    mixed,
    grams,
    outgoing,
    incoming,
    halo_send,
    halo_recv,
    gram_send,
    gram_recv,
    tile_send,
    tile_recv,
):
    visit = lax.axis_index("visit")
    row = lax.axis_index("row")
    patch = lax.axis_index("patch")
    members = visits * rows_count
    me = visit * rows_count + row

    def member(step):
        other = lax.rem(me + step, members)
        return {"visit": lax.div(other, rows_count), "row": lax.rem(other, rows_count)}

    barrier = pltpu.get_barrier_semaphore()
    for step in range(1, members):
        pl.semaphore_signal(barrier, inc=1, device_id=member(step), device_id_type=MESH)
    stars = star_ref[0]
    grams[me] = lax.dot_general(
        stars,
        stars,
        (((1,), (1,)), ((), ())),
        precision=HIGHEST,
        preferred_element_type=jnp.float32,
    )
    pl.semaphore_wait(barrier, members - 1)
    edge = pl.multiple_of((1 - row) * (R_DEV - HALO), HALO)
    halo_copy = pltpu.make_async_remote_copy(
        src_ref=sum_ref.at[:, pl.ds(edge, HALO), :],
        dst_ref=halo,
        send_sem=halo_send,
        recv_sem=halo_recv,
        device_id={"row": 1 - row},
        device_id_type=MESH,
    )
    halo_copy.start()
    gram_copies = []
    for step in range(1, members):
        copy = pltpu.make_async_remote_copy(
            src_ref=grams.at[me],
            dst_ref=grams.at[me],
            send_sem=gram_send.at[step],
            recv_sem=gram_recv.at[step],
            device_id=member(step),
            device_id_type=MESH,
        )
        copy.start()
        gram_copies.append(copy)

    groups = visits * TILES_DEV
    z[OWN_K + PAIRS * HALO :, :] = jnp.zeros((ALL_K - OWN_K - PAIRS * HALO, groups * TW), jnp.bfloat16)
    tap = iota((NTAPS, 2 * TW), 0)
    lanes = iota((NTAPS, 2 * TW), 1)
    near = (lanes == jnp.bitwise_and(-tap, 2 * TW - 1)).astype(jnp.float32)
    far = (lanes == jnp.bitwise_and(-1 - tap, 2 * TW - 1)).astype(jnp.float32)
    reversed_taps = jnp.dot(
        column_tap_ref[...].astype(jnp.float32), 0.375 * near + 0.625 * far, precision=HIGHEST
    )
    for b in range(NBASIS):
        base = jnp.broadcast_to(reversed_taps[b : b + 1, :], (2 * TW, 2 * TW))
        rolled = pltpu.roll(base, 0, 1, stride=1, stride_axis=0)
        band[:, b * TW : (b + 1) * TW] = rolled[:, 0:TW].astype(jnp.bfloat16)

    @pl.loop(0, groups)
    def _(group):
        at = pl.ds(pl.multiple_of(group * TW, TW), TW)
        for k in range(SLABS):
            out = jnp.dot(
                sum_ref[group * SLABS + k], band[...], preferred_element_type=jnp.float32
            ).astype(jnp.bfloat16)
            for b in range(NBASIS):
                m = k * NBASIS + b
                z[m * R_DEV : (m + 1) * R_DEV, at] = out[:, b * TW : (b + 1) * TW]

    halo_copy.wait_recv()

    @pl.loop(0, groups)
    def _(group):
        at = pl.ds(pl.multiple_of(group * TW, TW), TW)
        for k in range(SLABS):
            out = jnp.dot(
                halo[group * SLABS + k], band[...], preferred_element_type=jnp.float32
            ).astype(jnp.bfloat16)
            for b in range(NBASIS):
                m = k * NBASIS + b
                z[OWN_K + m * HALO : OWN_K + (m + 1) * HALO, at] = out[:, b * TW : (b + 1) * TW]

    for copy in gram_copies:
        copy.wait_recv()
    gram = grams[0]
    for s in range(1, members):
        gram = gram + grams[s]
    lower, solved = factor_steps(gram, stars)
    root = math.sqrt(star_total)
    factor = lower / root
    factor_ref[0] = factor
    white_ref[0] = solved * root
    eye = iota((NCOMP, NCOMP), 0) == iota((NCOMP, NCOMP), 1)
    diag = jnp.sum(jnp.where(eye, factor, 0.0), axis=1, keepdims=True)[:NBASIS]
    scale = diag / jnp.sqrt(jnp.sum(diag * diag, axis=0, keepdims=True) / NBASIS)
    sets = iota(coeff_ref.shape, 1)
    table = weight_ref[...].astype(jnp.float32)
    cell_visit, cell_ccd = iota(table.shape, 0), iota(table.shape, 1)

    def weight_of(source, k):
        hit = (cell_visit == source) & (cell_ccd == patch * C_DEV + k)
        return jnp.sum(jnp.where(hit, table, 0.0), keepdims=True)

    tap = iota((NTAPS, 2 * TW), 0)
    near = (lanes == jnp.bitwise_and(tap - HALF, 2 * TW - 1)).astype(jnp.float32)
    far = (lanes == jnp.bitwise_and(tap + 1 - HALF, 2 * TW - 1)).astype(jnp.float32)
    lane = iota((R_DEV, TW), 1)
    wide_sub = iota((R_DEV, 2 * TW), 0)
    last = (wide_sub == R_DEV - 1) & (row == rows_count - 1)
    halo_parts = [jnp.zeros((R_DEV, TW), jnp.float32) for _ in range(HALO_TILES)]
    for k in range(SLABS):
        picked = jnp.sum(
            jnp.where(sets == choice_ref[0, k], coeff_ref[...], 0.0), axis=1, keepdims=True
        )
        taps = (picked * scale) * row_tap_ref[...].astype(jnp.float32)
        taps = taps.astype(jnp.bfloat16).astype(jnp.float32)
        weight = weight_of(visit, k)
        first = jnp.dot(taps, near, precision=HIGHEST) * (0.75 * weight)
        second = jnp.dot(taps, far, precision=HIGHEST) * (0.25 * weight)
        for b in range(NBASIS):
            m = k * NBASIS + b
            one = jnp.broadcast_to(first[b : b + 1], (R_DEV, 2 * TW))
            two = jnp.broadcast_to(second[b : b + 1], (R_DEV, 2 * TW))
            base = one + jnp.where(last, 0.0, two)
            rolled = pltpu.roll(base, 0, 1, stride=1, stride_axis=0)
            mixed[:, m * TW : (m + 1) * TW] = rolled[:, 0:TW].astype(jnp.bfloat16)
            low = m % 8 * HALO
            piece = pltpu.roll(rolled[:, TW:], jnp.bitwise_and(low + row * HALO, TW - 1), 1)
            inside = (lane >= low) & (lane < low + HALO)
            halo_parts[m // 8] = jnp.where(inside, piece, halo_parts[m // 8])
    for t in range(HALO_TILES):
        mixed[:, OWN_K + t * TW : OWN_K + (t + 1) * TW] = halo_parts[t].astype(jnp.bfloat16)

    tile_copies = []
    for step in range(1, visits + 1):
        owner = lax.rem(visit + step, visits)
        at = pl.ds(pl.multiple_of(owner * TILES_DEV * TW, TILES_DEV * TW), TILES_DEV * TW)
        out = jnp.dot(mixed[...], z[:, at], preferred_element_type=jnp.float32)
        out = out.astype(jnp.bfloat16)
        for g in range(TILES_DEV):
            tile = out[:, g * TW : (g + 1) * TW]
            if step < visits:
                outgoing[step, g] = tile
            else:
                incoming[visit, g] = tile
        if step < visits:
            copy = pltpu.make_async_remote_copy(
                src_ref=outgoing.at[step],
                dst_ref=incoming.at[visit],
                send_sem=tile_send.at[step],
                recv_sem=tile_recv.at[step],
                device_id={"visit": owner},
                device_id_type=MESH,
            )
            copy.start()
            tile_copies.append(copy)

    slot_lane = iota((1, list_vec.shape[3]), 1)
    mine = (slot_lane >= visit * CAP) & (slot_lane < visit * CAP + CAP)
    totals = [jnp.zeros((1, 1), jnp.float32) for _ in range(TILES_DEV)]
    for s in range(visits):
        block, slot = list_vec[0, s], list_vec[2, s]
        for g in range(TILES_DEV):
            for k in range(SLABS):
                hits = jnp.where(mine & (block == k) & (slot == g), 1.0, 0.0)
                count = jnp.sum(hits, axis=1, keepdims=True)
                totals[g] = totals[g] + count * weight_of(s, k)
    for copy in tile_copies:
        copy.wait_recv()
    for g in range(TILES_DEV):
        numerator = incoming[0, g].astype(jnp.float32)
        for s in range(1, visits):
            numerator = numerator + incoming[s, g].astype(jnp.float32)
        coadd_ref[0, g] = numerator / totals[g]
    for copy in [halo_copy] + gram_copies + tile_copies:
        copy.wait_send()


def on_device(
    exposures,
    kernel_choice,
    kernel_coeffs,
    row_taps,
    column_taps,
    visit_weight,
    footprints,
    star_coeffs,
):
    visits = lax.axis_size("visit")
    rows_count = lax.axis_size("row")
    members = visits * rows_count
    groups = visits * TILES_DEV
    star_total = star_coeffs.shape[2] * members
    vmem = pl.BlockSpec(memory_space=pltpu.VMEM)
    smem = pl.BlockSpec(memory_space=pltpu.SMEM)
    tiles = pltpu.VMEM((visits, TILES_DEV, R_DEV, TW), jnp.bfloat16)
    dma = pltpu.SemaphoreType.DMA
    sums_shape = (groups * SLABS, R_DEV, 2 * TW)
    sums = pl.pallas_call(
        window_kernel,
        out_shape=jax.ShapeDtypeStruct(sums_shape, jnp.bfloat16),
        in_specs=[smem, pl.BlockSpec(memory_space=pl.ANY)],
        out_specs=vmem,
        scratch_shapes=[
            pltpu.VMEM((SLABS, R_DEV, CW + 2 * PAD), jnp.bfloat16),
            pltpu.VMEM(sums_shape, jnp.float32),
            dma((SLABS,)),
        ],
        compiler_params=pltpu.CompilerParams(vmem_limit_bytes=VMEM_LIMIT),
        name="windows",
    )(footprints, exposures)
    return pl.pallas_call(
        functools.partial(fused_kernel, visits, rows_count, star_total),
        out_shape=(
            jax.ShapeDtypeStruct((1, TILES_DEV, R_DEV, TW), jnp.float32),
            jax.ShapeDtypeStruct((1, NCOMP, NCOMP), jnp.float32),
            jax.ShapeDtypeStruct(star_coeffs.shape, jnp.float32),
        ),
        in_specs=[smem] + [vmem] * 7,
        out_specs=(vmem, vmem, vmem),
        scratch_shapes=[
            pltpu.VMEM((groups * SLABS, HALO, 2 * TW), jnp.bfloat16),
            pltpu.VMEM((2 * TW, NBASIS * TW), jnp.bfloat16),
            pltpu.VMEM((ALL_K, groups * TW), jnp.bfloat16),
            pltpu.VMEM((R_DEV, ALL_K), jnp.bfloat16),
            pltpu.VMEM((members, NCOMP, NCOMP), jnp.float32),
            tiles,
            tiles,
            dma,
            dma,
            dma((members,)),
            dma((members,)),
            dma((visits,)),
            dma((visits,)),
        ],
        compiler_params=pltpu.CompilerParams(
            vmem_limit_bytes=VMEM_LIMIT, collective_id=0, has_side_effects=True
        ),
        name="coadd",
    )(
        kernel_choice,
        footprints,
        visit_weight,
        kernel_coeffs,
        row_taps,
        column_taps,
        star_coeffs,
        sums,
    )


def solution(mesh):
    in_specs = (
        P(("blk", "visit"), "patch", "row", None),
        P(("blk", "visit"), "patch"),
        P(),
        P(),
        P(),
        P("blk", None),
        P(None, "blk", "patch", None),
        P(("blk", "patch"), None, ("visit", "row")),
    )
    out_specs = (
        P(("blk", "patch"), "visit", "row", None),
        P(("blk", "patch"), None, None),
        P(("blk", "patch"), None, ("visit", "row")),
    )
    return jax.shard_map(
        on_device, mesh=mesh, in_specs=in_specs, out_specs=out_specs, check_vma=False
    )
```

```python
import functools
import math

import jax
import jax.numpy as jnp
from jax import lax
from jax.experimental import pallas as pl
from jax.experimental.pallas import tpu as pltpu
from jax.sharding import PartitionSpec as P

NBASIS = 9
NTAPS = 21
C_DEV = 2
R_DEV = 128
CW = 4096
TW = 128
CAP = 8
TILES_DEV = 2
HALF = 10
SLABS = 2
HALO = 16
NCOMP = 32
PAD = 128
PAIRS = SLABS * NBASIS
OWN_K = PAIRS * R_DEV
HALO_TILES = 3
BATCH = 4
ALL_K = OWN_K + HALO_TILES * TW
HIGHEST = lax.Precision.HIGHEST
VMEM_LIMIT = 60 * 1024 * 1024
MESH = pl.DeviceIdType.MESH


def iota(shape, axis):
    return lax.broadcasted_iota(jnp.int32, shape, axis)


def window_kernel(list_ref, image_ref, sum_ref, padded, sums, sem):
    visit = lax.axis_index("visit")
    slots = list_ref.shape[3]
    loads = []
    for k in range(SLABS):
        copy = pltpu.make_async_copy(image_ref.at[0, k], padded.at[k, :, PAD : PAD + CW], sem.at[k])
        copy.start()
        loads.append(copy)
    for k in range(SLABS):
        padded[k, :, 0:PAD] = jnp.zeros((R_DEV, PAD), jnp.bfloat16)
        padded[k, :, PAD + CW :] = jnp.zeros((R_DEV, PAD), jnp.bfloat16)
    sums[...] = jnp.zeros_like(sums)
    lane = iota((R_DEV, TW), 1)
    for copy in loads:
        copy.wait()

    @pl.loop(0, slots)
    def _(q):
        k = list_ref[0, visit, 0, q]

        @pl.when(k >= 0)
        def _():
            start = list_ref[1, visit, 0, q] + (PAD - HALF)
            tile = lax.shift_right_logical(start, 7)
            shift = start - tile * TW
            back = jnp.bitwise_and(TW - shift, TW - 1)
            place = (lax.div(q, CAP) * TILES_DEV + list_ref[2, visit, 0, q]) * SLABS + k
            parts = []
            for t in range(3):
                at = pl.multiple_of((tile + t) * TW, TW)
                parts.append(pltpu.roll(padded[k, :, pl.ds(at, TW)].astype(jnp.float32), back, 1))
            keep = lane < TW - shift
            sums[place, :, 0:TW] += jnp.where(keep, parts[0], parts[1])
            sums[place, :, TW : 2 * TW] += jnp.where(keep, parts[1], parts[2])

    @pl.loop(0, sums.shape[0])
    def _(place):
        sum_ref[place] = sums[place].astype(jnp.bfloat16)


def factor_steps(gram, stars):
    sub = lax.broadcasted_iota(jnp.int32, (NCOMP, 1), 0)
    lane = lax.broadcasted_iota(jnp.int32, (NCOMP, NCOMP), 1)
    lower = jnp.zeros((NCOMP, NCOMP), jnp.float32)
    for j in range(NCOMP):
        inv = 1.0 / jnp.sqrt(gram[j : j + 1, j : j + 1])
        column = gram[:, j : j + 1] * inv
        lower = jnp.where((lane == j) & (sub >= j), column, lower)
        below = jnp.where(sub > j, column, 0.0)
        solved = stars[j : j + 1, :] * inv
        gram = gram - below * (gram[j : j + 1, :] * inv)
        stars = jnp.where(sub == j, solved, stars - below * solved)
    return lower, stars


def fused_kernel(
    visits,
    rows_count,
    star_total,
    choice_ref,
    list_vec,
    weight_ref,
    coeff_ref,
    row_tap_ref,
    column_tap_ref,
    star_ref,
    sum_ref,
    coadd_ref,
    factor_ref,
    white_ref,
    halo,
    band,
    z,
    mixed,
    grams,
    outgoing,
    incoming,
    halo_send,
    halo_recv,
    gram_send,
    gram_recv,
    tile_send,
    tile_recv,
):
    visit = lax.axis_index("visit")
    row = lax.axis_index("row")
    patch = lax.axis_index("patch")
    members = visits * rows_count
    me = visit * rows_count + row

    def member(step):
        other = lax.rem(me + step, members)
        return {"visit": lax.div(other, rows_count), "row": lax.rem(other, rows_count)}

    barrier = pltpu.get_barrier_semaphore()
    for step in range(1, members):
        pl.semaphore_signal(barrier, inc=1, device_id=member(step), device_id_type=MESH)
    stars = star_ref[0]
    grams[me] = lax.dot_general(
        stars,
        stars,
        (((1,), (1,)), ((), ())),
        precision=HIGHEST,
        preferred_element_type=jnp.float32,
    )
    pl.semaphore_wait(barrier, members - 1)
    edge = pl.multiple_of((1 - row) * (R_DEV - HALO), HALO)
    halo_copy = pltpu.make_async_remote_copy(
        src_ref=sum_ref.at[:, pl.ds(edge, HALO), :],
        dst_ref=halo,
        send_sem=halo_send,
        recv_sem=halo_recv,
        device_id={"row": 1 - row},
        device_id_type=MESH,
    )
    halo_copy.start()
    gram_copies = []
    for step in range(1, members):
        copy = pltpu.make_async_remote_copy(
            src_ref=grams.at[me],
            dst_ref=grams.at[me],
            send_sem=gram_send.at[step],
            recv_sem=gram_recv.at[step],
            device_id=member(step),
            device_id_type=MESH,
        )
        copy.start()
        gram_copies.append(copy)

    groups = visits * TILES_DEV
    z[OWN_K + PAIRS * HALO :, :] = jnp.zeros((ALL_K - OWN_K - PAIRS * HALO, groups * TW), jnp.bfloat16)
    tap = iota((NTAPS, 2 * TW), 0)
    lanes = iota((NTAPS, 2 * TW), 1)
    near = (lanes == jnp.bitwise_and(-tap, 2 * TW - 1)).astype(jnp.float32)
    far = (lanes == jnp.bitwise_and(-1 - tap, 2 * TW - 1)).astype(jnp.float32)
    reversed_taps = jnp.dot(
        column_tap_ref[...].astype(jnp.float32), 0.375 * near + 0.625 * far, precision=HIGHEST
    )
    for b in range(NBASIS):
        base = jnp.broadcast_to(reversed_taps[b : b + 1, :], (2 * TW, 2 * TW))
        rolled = pltpu.roll(base, 0, 1, stride=1, stride_axis=0)
        band[:, b * TW : (b + 1) * TW] = rolled[:, 0:TW].astype(jnp.bfloat16)

    def store(out, place, count, first_row):
        group, k = place
        at = pl.ds(pl.multiple_of(group * TW, TW), TW)
        for b in range(NBASIS):
            z[pl.ds(first_row + (k * NBASIS + b) * count, count), at] = out[:, b * TW : (b + 1) * TW]

    def filter_own(step):
        block = sum_ref[pl.ds(step * BATCH, BATCH)].reshape(BATCH * R_DEV, 2 * TW)
        out = jnp.dot(block, band[...], preferred_element_type=jnp.float32).astype(jnp.bfloat16)
        for c in range(BATCH):
            group = step * (BATCH // SLABS) + c // SLABS
            store(out[c * R_DEV : (c + 1) * R_DEV], (group, c % SLABS), R_DEV, 0)

    for copy in gram_copies:
        copy.wait_recv()
    halo_copy.wait_recv()
    gram = grams[0]
    for s in range(1, members):
        gram = gram + grams[s]
    places = groups * SLABS
    block = halo[...].reshape(places * HALO, 2 * TW)
    out = jnp.dot(block, band[...], preferred_element_type=jnp.float32).astype(jnp.bfloat16)
    for place in range(places):
        store(out[place * HALO : (place + 1) * HALO], (place // SLABS, place % SLABS), HALO, OWN_K)
    steps = places // BATCH
    unrolled = min(steps, 4)
    for step in range(unrolled):
        filter_own(step)
    lower, solved = factor_steps(gram, stars)
    if steps > unrolled:
        pl.loop(unrolled, steps)(filter_own)
    root = math.sqrt(star_total)
    factor = lower / root
    factor_ref[0] = factor
    white_ref[0] = solved * root
    eye = iota((NCOMP, NCOMP), 0) == iota((NCOMP, NCOMP), 1)
    diag = jnp.sum(jnp.where(eye, factor, 0.0), axis=1, keepdims=True)[:NBASIS]
    scale = diag / jnp.sqrt(jnp.sum(diag * diag, axis=0, keepdims=True) / NBASIS)
    sets = iota(coeff_ref.shape, 1)
    table = weight_ref[...].astype(jnp.float32)
    cell_visit, cell_ccd = iota(table.shape, 0), iota(table.shape, 1)

    def weight_of(source, k):
        hit = (cell_visit == source) & (cell_ccd == patch * C_DEV + k)
        return jnp.sum(jnp.where(hit, table, 0.0), keepdims=True)

    tap = iota((NTAPS, 2 * TW), 0)
    near = (lanes == jnp.bitwise_and(tap - HALF, 2 * TW - 1)).astype(jnp.float32)
    far = (lanes == jnp.bitwise_and(tap + 1 - HALF, 2 * TW - 1)).astype(jnp.float32)
    lane = iota((R_DEV, TW), 1)
    wide_sub = iota((R_DEV, 2 * TW), 0)
    last = (wide_sub == R_DEV - 1) & (row == rows_count - 1)
    halo_parts = [jnp.zeros((R_DEV, TW), jnp.float32) for _ in range(HALO_TILES)]
    for k in range(SLABS):
        picked = jnp.sum(
            jnp.where(sets == choice_ref[0, k], coeff_ref[...], 0.0), axis=1, keepdims=True
        )
        taps = (picked * scale) * row_tap_ref[...].astype(jnp.float32)
        taps = taps.astype(jnp.bfloat16).astype(jnp.float32)
        weight = weight_of(visit, k)
        first = jnp.dot(taps, near, precision=HIGHEST) * (0.75 * weight)
        second = jnp.dot(taps, far, precision=HIGHEST) * (0.25 * weight)
        for b in range(NBASIS):
            m = k * NBASIS + b
            one = jnp.broadcast_to(first[b : b + 1], (R_DEV, 2 * TW))
            two = jnp.broadcast_to(second[b : b + 1], (R_DEV, 2 * TW))
            base = one + jnp.where(last, 0.0, two)
            rolled = pltpu.roll(base, 0, 1, stride=1, stride_axis=0)
            mixed[:, m * TW : (m + 1) * TW] = rolled[:, 0:TW].astype(jnp.bfloat16)
            low = m % 8 * HALO
            piece = pltpu.roll(rolled[:, TW:], jnp.bitwise_and(low + row * HALO, TW - 1), 1)
            inside = (lane >= low) & (lane < low + HALO)
            halo_parts[m // 8] = jnp.where(inside, piece, halo_parts[m // 8])
    for t in range(HALO_TILES):
        mixed[:, OWN_K + t * TW : OWN_K + (t + 1) * TW] = halo_parts[t].astype(jnp.bfloat16)

    tile_copies = []
    for step in range(1, visits + 1):
        owner = lax.rem(visit + step, visits)
        at = pl.ds(pl.multiple_of(owner * TILES_DEV * TW, TILES_DEV * TW), TILES_DEV * TW)
        out = jnp.dot(mixed[...], z[:, at], preferred_element_type=jnp.float32)
        out = out.astype(jnp.bfloat16)
        for g in range(TILES_DEV):
            tile = out[:, g * TW : (g + 1) * TW]
            if step < visits:
                outgoing[step, g] = tile
            else:
                incoming[visit, g] = tile
        if step < visits:
            copy = pltpu.make_async_remote_copy(
                src_ref=outgoing.at[step],
                dst_ref=incoming.at[visit],
                send_sem=tile_send.at[step],
                recv_sem=tile_recv.at[step],
                device_id={"visit": owner},
                device_id_type=MESH,
            )
            copy.start()
            tile_copies.append(copy)

    slot_lane = iota((1, list_vec.shape[3]), 1)
    mine = (slot_lane >= visit * CAP) & (slot_lane < visit * CAP + CAP)
    totals = [jnp.zeros((1, 1), jnp.float32) for _ in range(TILES_DEV)]
    for s in range(visits):
        block, slot = list_vec[0, s], list_vec[2, s]
        for g in range(TILES_DEV):
            for k in range(SLABS):
                hits = jnp.where(mine & (block == k) & (slot == g), 1.0, 0.0)
                count = jnp.sum(hits, axis=1, keepdims=True)
                totals[g] = totals[g] + count * weight_of(s, k)
    for copy in tile_copies:
        copy.wait_recv()
    for g in range(TILES_DEV):
        numerator = incoming[0, g].astype(jnp.float32)
        for s in range(1, visits):
            numerator = numerator + incoming[s, g].astype(jnp.float32)
        coadd_ref[0, g] = numerator / totals[g]
    for copy in [halo_copy] + gram_copies + tile_copies:
        copy.wait_send()


def result_kernel(*refs):
    for source, target in zip(refs[:3], refs[3:]):
        target[...] = source[...]


def on_device(
    exposures,
    kernel_choice,
    kernel_coeffs,
    row_taps,
    column_taps,
    visit_weight,
    footprints,
    star_coeffs,
):
    visits = lax.axis_size("visit")
    rows_count = lax.axis_size("row")
    members = visits * rows_count
    groups = visits * TILES_DEV
    star_total = star_coeffs.shape[2] * members
    vmem = pl.BlockSpec(memory_space=pltpu.VMEM)
    smem = pl.BlockSpec(memory_space=pltpu.SMEM)
    tiles = pltpu.VMEM((visits, TILES_DEV, R_DEV, TW), jnp.bfloat16)
    dma = pltpu.SemaphoreType.DMA
    sums_shape = (groups * SLABS, R_DEV, 2 * TW)
    sums = pl.pallas_call(
        window_kernel,
        out_shape=jax.ShapeDtypeStruct(sums_shape, jnp.bfloat16),
        in_specs=[smem, pl.BlockSpec(memory_space=pl.ANY)],
        out_specs=vmem,
        scratch_shapes=[
            pltpu.VMEM((SLABS, R_DEV, CW + 2 * PAD), jnp.bfloat16),
            pltpu.VMEM(sums_shape, jnp.float32),
            dma((SLABS,)),
        ],
        compiler_params=pltpu.CompilerParams(vmem_limit_bytes=VMEM_LIMIT),
        name="windows",
    )(footprints, exposures)
    results = pl.pallas_call(
        functools.partial(fused_kernel, visits, rows_count, star_total),
        out_shape=(
            jax.ShapeDtypeStruct((1, TILES_DEV, R_DEV, TW), jnp.float32),
            jax.ShapeDtypeStruct((1, NCOMP, NCOMP), jnp.float32),
            jax.ShapeDtypeStruct(star_coeffs.shape, jnp.float32),
        ),
        in_specs=[smem] + [vmem] * 7,
        out_specs=(vmem, vmem, vmem),
        scratch_shapes=[
            pltpu.VMEM((groups * SLABS, HALO, 2 * TW), jnp.bfloat16),
            pltpu.VMEM((2 * TW, NBASIS * TW), jnp.bfloat16),
            pltpu.VMEM((ALL_K, groups * TW), jnp.bfloat16),
            pltpu.VMEM((R_DEV, ALL_K), jnp.bfloat16),
            pltpu.VMEM((members, NCOMP, NCOMP), jnp.float32),
            tiles,
            tiles,
            dma,
            dma,
            dma((members,)),
            dma((members,)),
            dma((visits,)),
            dma((visits,)),
        ],
        compiler_params=pltpu.CompilerParams(
            vmem_limit_bytes=VMEM_LIMIT, collective_id=0, has_side_effects=True
        ),
        name="coadd",
    )(
        kernel_choice,
        footprints,
        visit_weight,
        kernel_coeffs,
        row_taps,
        column_taps,
        star_coeffs,
        sums,
    )
    return pl.pallas_call(
        result_kernel,
        out_shape=tuple(jax.ShapeDtypeStruct(part.shape, part.dtype) for part in results),
        in_specs=[vmem] * 3,
        out_specs=(vmem,) * 3,
        name="results",
    )(*results)


def solution(mesh):
    in_specs = (
        P(("blk", "visit"), "patch", "row", None),
        P(("blk", "visit"), "patch"),
        P(),
        P(),
        P(),
        P("blk", None),
        P(None, "blk", "patch", None),
        P(("blk", "patch"), None, ("visit", "row")),
    )
    out_specs = (
        P(("blk", "patch"), "visit", "row", None),
        P(("blk", "patch"), None, None),
        P(("blk", "patch"), None, ("visit", "row")),
    )
    return jax.shard_map(
        on_device, mesh=mesh, in_specs=in_specs, out_specs=out_specs, check_vma=False
    )
```

```python
import functools
import math

import jax
import jax.numpy as jnp
from jax import lax
from jax.experimental import pallas as pl
from jax.experimental.pallas import tpu as pltpu
from jax.sharding import PartitionSpec as P

NBASIS = 9
NTAPS = 21
C_DEV = 2
R_DEV = 128
CW = 4096
TW = 128
CAP = 8
TILES_DEV = 2
HALF = 10
SLABS = 2
HALO = 16
NCOMP = 32
PAD = 128
PAIRS = SLABS * NBASIS
OWN_K = PAIRS * R_DEV
HALO_TILES = 3
BATCH = 4
ALL_K = OWN_K + HALO_TILES * TW
HIGHEST = lax.Precision.HIGHEST
VMEM_LIMIT = 60 * 1024 * 1024
MESH = pl.DeviceIdType.MESH


def iota(shape, axis):
    return lax.broadcasted_iota(jnp.int32, shape, axis)


def window_kernel(list_ref, image_ref, sum_ref, padded, sums, sem):
    visit = lax.axis_index("visit")
    slots = list_ref.shape[3]
    loads = []
    for k in range(SLABS):
        copy = pltpu.make_async_copy(image_ref.at[0, k], padded.at[k, :, PAD : PAD + CW], sem.at[k])
        copy.start()
        loads.append(copy)
    for k in range(SLABS):
        padded[k, :, 0:PAD] = jnp.zeros((R_DEV, PAD), jnp.bfloat16)
        padded[k, :, PAD + CW :] = jnp.zeros((R_DEV, PAD), jnp.bfloat16)
    sums[...] = jnp.zeros_like(sums)
    lane = iota((R_DEV, TW), 1)
    for copy in loads:
        copy.wait()

    @pl.loop(0, slots)
    def _(q):
        k = list_ref[0, visit, 0, q]

        @pl.when(k >= 0)
        def _():
            start = list_ref[1, visit, 0, q] + (PAD - HALF)
            tile = lax.shift_right_logical(start, 7)
            shift = start - tile * TW
            back = jnp.bitwise_and(TW - shift, TW - 1)
            place = (lax.div(q, CAP) * TILES_DEV + list_ref[2, visit, 0, q]) * SLABS + k
            parts = []
            for t in range(3):
                at = pl.multiple_of((tile + t) * TW, TW)
                parts.append(pltpu.roll(padded[k, :, pl.ds(at, TW)].astype(jnp.float32), back, 1))
            keep = lane < TW - shift
            sums[place, :, 0:TW] += jnp.where(keep, parts[0], parts[1])
            sums[place, :, TW : 2 * TW] += jnp.where(keep, parts[1], parts[2])

    @pl.loop(0, sums.shape[0])
    def _(place):
        sum_ref[place] = sums[place].astype(jnp.bfloat16)


def factor_steps(gram, stars):
    sub = lax.broadcasted_iota(jnp.int32, (NCOMP, 1), 0)
    lane = lax.broadcasted_iota(jnp.int32, (NCOMP, NCOMP), 1)
    lower = jnp.zeros((NCOMP, NCOMP), jnp.float32)
    for j in range(NCOMP):
        column = gram[:, j : j + 1]
        below = jnp.where(sub > j, column / gram[j : j + 1, j : j + 1], 0.0)
        lower = jnp.where((lane == j) & (sub >= j), column, lower)
        gram = gram - below * gram[j : j + 1, :]
        stars = stars - below * stars[j : j + 1, :]
    pivots = jnp.where(lane == sub, lower, 0.0)
    lower = lower / jnp.sqrt(jnp.sum(pivots, axis=0, keepdims=True))
    stars = stars / jnp.sqrt(jnp.sum(pivots, axis=1, keepdims=True))
    return lower, stars


def fused_kernel(
    visits,
    rows_count,
    star_total,
    choice_ref,
    list_vec,
    weight_ref,
    coeff_ref,
    row_tap_ref,
    column_tap_ref,
    star_ref,
    sum_ref,
    coadd_ref,
    factor_ref,
    white_ref,
    halo,
    band,
    z,
    mixed,
    grams,
    outgoing,
    incoming,
    halo_send,
    halo_recv,
    gram_send,
    gram_recv,
    tile_send,
    tile_recv,
):
    visit = lax.axis_index("visit")
    row = lax.axis_index("row")
    patch = lax.axis_index("patch")
    members = visits * rows_count
    me = visit * rows_count + row

    def member(step):
        other = lax.rem(me + step, members)
        return {"visit": lax.div(other, rows_count), "row": lax.rem(other, rows_count)}

    barrier = pltpu.get_barrier_semaphore()
    for step in range(1, members):
        pl.semaphore_signal(barrier, inc=1, device_id=member(step), device_id_type=MESH)
    stars = star_ref[0]
    grams[me] = lax.dot_general(
        stars,
        stars,
        (((1,), (1,)), ((), ())),
        precision=HIGHEST,
        preferred_element_type=jnp.float32,
    )
    pl.semaphore_wait(barrier, members - 1)
    edge = pl.multiple_of((1 - row) * (R_DEV - HALO), HALO)
    halo_copy = pltpu.make_async_remote_copy(
        src_ref=sum_ref.at[:, pl.ds(edge, HALO), :],
        dst_ref=halo,
        send_sem=halo_send,
        recv_sem=halo_recv,
        device_id={"row": 1 - row},
        device_id_type=MESH,
    )
    halo_copy.start()
    gram_copies = []
    for step in range(1, members):
        copy = pltpu.make_async_remote_copy(
            src_ref=grams.at[me],
            dst_ref=grams.at[me],
            send_sem=gram_send.at[step],
            recv_sem=gram_recv.at[step],
            device_id=member(step),
            device_id_type=MESH,
        )
        copy.start()
        gram_copies.append(copy)

    groups = visits * TILES_DEV
    z[OWN_K + PAIRS * HALO :, :] = jnp.zeros((ALL_K - OWN_K - PAIRS * HALO, groups * TW), jnp.bfloat16)
    tap = iota((NTAPS, TW), 0)
    lanes = iota((NTAPS, TW), 1)
    near = (lanes == jnp.bitwise_and(-tap, TW - 1)).astype(jnp.float32)
    far = (lanes == jnp.bitwise_and(-1 - tap, TW - 1)).astype(jnp.float32)
    reversed_taps = jnp.dot(
        column_tap_ref[...].astype(jnp.float32), 0.375 * near + 0.625 * far, precision=HIGHEST
    )
    sub_index, lane = iota((TW, TW), 0), iota((TW, TW), 1)
    for b in range(NBASIS):
        base = jnp.broadcast_to(reversed_taps[b : b + 1, :], (TW, TW))
        rolled = pltpu.roll(base, 0, 1, stride=1, stride_axis=0)
        at = slice(b * TW, (b + 1) * TW)
        band[0:TW, at] = jnp.where(lane <= sub_index, rolled, 0.0).astype(jnp.bfloat16)
        band[TW : 2 * TW, at] = jnp.where(lane > sub_index, rolled, 0.0).astype(jnp.bfloat16)

    def store(out, place, count, first_row):
        group, k = place
        at = pl.ds(pl.multiple_of(group * TW, TW), TW)
        for b in range(NBASIS):
            z[pl.ds(first_row + (k * NBASIS + b) * count, count), at] = out[:, b * TW : (b + 1) * TW]

    def filter_own(step):
        block = sum_ref[pl.ds(step * BATCH, BATCH)].reshape(BATCH * R_DEV, 2 * TW)
        out = jnp.dot(block, band[...], preferred_element_type=jnp.float32).astype(jnp.bfloat16)
        for c in range(BATCH):
            group = step * (BATCH // SLABS) + c // SLABS
            store(out[c * R_DEV : (c + 1) * R_DEV], (group, c % SLABS), R_DEV, 0)

    for copy in gram_copies:
        copy.wait_recv()
    halo_copy.wait_recv()
    gram = grams[0]
    for s in range(1, members):
        gram = gram + grams[s]
    places = groups * SLABS
    block = halo[...].reshape(places * HALO, 2 * TW)
    out = jnp.dot(block, band[...], preferred_element_type=jnp.float32).astype(jnp.bfloat16)
    for place in range(places):
        store(out[place * HALO : (place + 1) * HALO], (place // SLABS, place % SLABS), HALO, OWN_K)
    steps = places // BATCH
    unrolled = min(steps, 4)
    for step in range(unrolled):
        filter_own(step)
    lower, solved = factor_steps(gram, stars)
    if steps > unrolled:
        pl.loop(unrolled, steps)(filter_own)
    root = math.sqrt(star_total)
    factor = lower / root
    factor_ref[0] = factor
    white_ref[0] = solved * root
    eye = iota((NCOMP, NCOMP), 0) == iota((NCOMP, NCOMP), 1)
    diag = jnp.sum(jnp.where(eye, factor, 0.0), axis=1, keepdims=True)[:NBASIS]
    scale = diag / jnp.sqrt(jnp.sum(diag * diag, axis=0, keepdims=True) / NBASIS)
    sets = iota(coeff_ref.shape, 1)
    table = weight_ref[...].astype(jnp.float32)
    cell_visit, cell_ccd = iota(table.shape, 0), iota(table.shape, 1)

    def weight_of(source, k):
        hit = (cell_visit == source) & (cell_ccd == patch * C_DEV + k)
        return jnp.sum(jnp.where(hit, table, 0.0), keepdims=True)

    near = (lanes == jnp.bitwise_and(tap - HALF, TW - 1)).astype(jnp.float32)
    far = (lanes == jnp.bitwise_and(tap + 1 - HALF, TW - 1)).astype(jnp.float32)
    last = (sub_index == R_DEV - 1) & (row == rows_count - 1)
    ahead = lane - sub_index
    own = (ahead > -TW // 2) & (ahead < TW // 2)
    beyond = ahead * (2 * row - 1) >= TW // 2
    halo_parts = [jnp.zeros((R_DEV, TW), jnp.float32) for _ in range(HALO_TILES)]
    for k in range(SLABS):
        picked = jnp.sum(
            jnp.where(sets == choice_ref[0, k], coeff_ref[...], 0.0), axis=1, keepdims=True
        )
        taps = (picked * scale) * row_tap_ref[...].astype(jnp.float32)
        taps = taps.astype(jnp.bfloat16).astype(jnp.float32)
        weight = weight_of(visit, k)
        first = jnp.dot(taps, near, precision=HIGHEST) * (0.75 * weight)
        second = jnp.dot(taps, far, precision=HIGHEST) * (0.25 * weight)
        for b in range(NBASIS):
            m = k * NBASIS + b
            one = jnp.broadcast_to(first[b : b + 1], (R_DEV, TW))
            two = jnp.broadcast_to(second[b : b + 1], (R_DEV, TW))
            base = one + jnp.where(last, 0.0, two)
            rolled = pltpu.roll(base, 0, 1, stride=1, stride_axis=0)
            mixed[:, m * TW : (m + 1) * TW] = jnp.where(own, rolled, 0.0).astype(jnp.bfloat16)
            low = m % 8 * HALO
            piece = jnp.where(beyond, rolled, 0.0)
            piece = pltpu.roll(piece, jnp.bitwise_and(low + row * HALO, TW - 1), 1)
            inside = (lane >= low) & (lane < low + HALO)
            halo_parts[m // 8] = jnp.where(inside, piece, halo_parts[m // 8])
    for t in range(HALO_TILES):
        mixed[:, OWN_K + t * TW : OWN_K + (t + 1) * TW] = halo_parts[t].astype(jnp.bfloat16)

    tile_copies = []
    for step in range(1, visits + 1):
        owner = lax.rem(visit + step, visits)
        at = pl.ds(pl.multiple_of(owner * TILES_DEV * TW, TILES_DEV * TW), TILES_DEV * TW)
        out = jnp.dot(mixed[...], z[:, at], preferred_element_type=jnp.float32)
        out = out.astype(jnp.bfloat16)
        for g in range(TILES_DEV):
            tile = out[:, g * TW : (g + 1) * TW]
            if step < visits:
                outgoing[step, g] = tile
            else:
                incoming[visit, g] = tile
        if step < visits:
            copy = pltpu.make_async_remote_copy(
                src_ref=outgoing.at[step],
                dst_ref=incoming.at[visit],
                send_sem=tile_send.at[step],
                recv_sem=tile_recv.at[step],
                device_id={"visit": owner},
                device_id_type=MESH,
            )
            copy.start()
            tile_copies.append(copy)

    slot_lane = iota((1, list_vec.shape[3]), 1)
    mine = (slot_lane >= visit * CAP) & (slot_lane < visit * CAP + CAP)
    totals = [jnp.zeros((1, 1), jnp.float32) for _ in range(TILES_DEV)]
    for s in range(visits):
        block, slot = list_vec[0, s], list_vec[2, s]
        for g in range(TILES_DEV):
            for k in range(SLABS):
                hits = jnp.where(mine & (block == k) & (slot == g), 1.0, 0.0)
                count = jnp.sum(hits, axis=1, keepdims=True)
                totals[g] = totals[g] + count * weight_of(s, k)
    for copy in tile_copies:
        copy.wait_recv()
    for g in range(TILES_DEV):
        numerator = incoming[0, g].astype(jnp.float32)
        for s in range(1, visits):
            numerator = numerator + incoming[s, g].astype(jnp.float32)
        coadd_ref[0, g] = numerator / totals[g]
    for copy in [halo_copy] + gram_copies + tile_copies:
        copy.wait_send()


def result_kernel(*refs):
    for source, target in zip(refs[:3], refs[3:]):
        target[...] = source[...]


def on_device(
    exposures,
    kernel_choice,
    kernel_coeffs,
    row_taps,
    column_taps,
    visit_weight,
    footprints,
    star_coeffs,
):
    visits = lax.axis_size("visit")
    rows_count = lax.axis_size("row")
    members = visits * rows_count
    groups = visits * TILES_DEV
    star_total = star_coeffs.shape[2] * members
    vmem = pl.BlockSpec(memory_space=pltpu.VMEM)
    smem = pl.BlockSpec(memory_space=pltpu.SMEM)
    tiles = pltpu.VMEM((visits, TILES_DEV, R_DEV, TW), jnp.bfloat16)
    dma = pltpu.SemaphoreType.DMA
    sums_shape = (groups * SLABS, R_DEV, 2 * TW)
    sums = pl.pallas_call(
        window_kernel,
        out_shape=jax.ShapeDtypeStruct(sums_shape, jnp.bfloat16),
        in_specs=[smem, pl.BlockSpec(memory_space=pl.ANY)],
        out_specs=vmem,
        scratch_shapes=[
            pltpu.VMEM((SLABS, R_DEV, CW + 2 * PAD), jnp.bfloat16),
            pltpu.VMEM(sums_shape, jnp.float32),
            dma((SLABS,)),
        ],
        compiler_params=pltpu.CompilerParams(vmem_limit_bytes=VMEM_LIMIT),
        name="windows",
    )(footprints, exposures)
    results = pl.pallas_call(
        functools.partial(fused_kernel, visits, rows_count, star_total),
        out_shape=(
            jax.ShapeDtypeStruct((1, TILES_DEV, R_DEV, TW), jnp.float32),
            jax.ShapeDtypeStruct((1, NCOMP, NCOMP), jnp.float32),
            jax.ShapeDtypeStruct(star_coeffs.shape, jnp.float32),
        ),
        in_specs=[smem] + [vmem] * 7,
        out_specs=(vmem, vmem, vmem),
        scratch_shapes=[
            pltpu.VMEM((groups * SLABS, HALO, 2 * TW), jnp.bfloat16),
            pltpu.VMEM((2 * TW, NBASIS * TW), jnp.bfloat16),
            pltpu.VMEM((ALL_K, groups * TW), jnp.bfloat16),
            pltpu.VMEM((R_DEV, ALL_K), jnp.bfloat16),
            pltpu.VMEM((members, NCOMP, NCOMP), jnp.float32),
            tiles,
            tiles,
            dma,
            dma,
            dma((members,)),
            dma((members,)),
            dma((visits,)),
            dma((visits,)),
        ],
        compiler_params=pltpu.CompilerParams(
            vmem_limit_bytes=VMEM_LIMIT, collective_id=0, has_side_effects=True
        ),
        name="coadd",
    )(
        kernel_choice,
        footprints,
        visit_weight,
        kernel_coeffs,
        row_taps,
        column_taps,
        star_coeffs,
        sums,
    )
    return pl.pallas_call(
        result_kernel,
        out_shape=tuple(jax.ShapeDtypeStruct(part.shape, part.dtype) for part in results),
        in_specs=[vmem] * 3,
        out_specs=(vmem,) * 3,
        name="results",
    )(*results)


def solution(mesh):
    in_specs = (
        P(("blk", "visit"), "patch", "row", None),
        P(("blk", "visit"), "patch"),
        P(),
        P(),
        P(),
        P("blk", None),
        P(None, "blk", "patch", None),
        P(("blk", "patch"), None, ("visit", "row")),
    )
    out_specs = (
        P(("blk", "patch"), "visit", "row", None),
        P(("blk", "patch"), None, None),
        P(("blk", "patch"), None, ("visit", "row")),
    )
    return jax.shard_map(
        on_device, mesh=mesh, in_specs=in_specs, out_specs=out_specs, check_vma=False
    )
```
